32 devices in a mesh: ctx: 4 (over y, x), exp: 8 (over z, core).
Axes of the slice: x: 2, y: 2, z: 4, core: 2. Of those that a mesh axis runs over, the one named last changes fastest.
Arguments:
- hidden_in: bfloat16 [1024, 2048], P(('ctx', 'exp')), may hold values from -6 to 6
- queries: bfloat16 [1024, 4096], P('ctx', 'exp'), may hold values from -200 to 200
- keyvals: bfloat16 [1024, 512], P('ctx'), may hold values from -6 to 6
- out_weight: bfloat16 [4096, 2048], P('exp'), may hold values from -0.09375 to 0.09375
- norm_gain: float32 [2048], replicated, may hold values from 0.5 to 1.5
- router_weight: bfloat16 [2048, 16], replicated, may hold values from -0.125 to 0.125
- expert_gate_up: bfloat16 [16, 2048, 1536], P('exp', 'ctx'), may hold values from -0.125 to 0.125
- expert_down: bfloat16 [16, 768, 2048], P('exp', 'ctx'), may hold values from -0.21875 to 0.21875
- route_ids: int32 [1024, 8], P(('ctx', 'exp')), may hold values from 0 to 15, all different within a row; in each aligned block of 32 rows (0 to 31, 32 to 63, ...) at most 18 rows name the same one
- upstream: bfloat16 [1024, 2048], P(('ctx', 'exp')), may hold values from -6 to 6
Outputs:
- layer_out: bfloat16 [1024, 2048], P(('ctx', 'exp'))
- input_grad: bfloat16 [1024, 2048], P(('ctx', 'exp'))
- query_grad: bfloat16 [1024, 4096], P('ctx', 'exp')
- out_weight_grad: float32 [4096, 2048], P('exp', 'ctx')
- gate_up_grad: float32 [16, 2048, 1536], P('exp', 'ctx')
- down_grad: float32 [16, 768, 2048], P('exp', 'ctx')
- router_grad: float32 [2048, 16], replicated
- gain_grad: float32 [2048], replicated
The draws below stay inside these ranges and needn't reach their ends.
Inputs may be any that keep to these rules, and one draw needn't show every extreme that they name: `route_ids`: each row names 8 different experts. In each aligned block of 32 rows (the rows of one device) no expert is named by more than 18 rows, a bound that some block reaches.
All inputs are finite; a program needn't handle non-finite values.
Results may differ from the reference program's by a relative error of at most 0.02.
Values may be sent and summed in bfloat16 or wider, within the bound.
A program may use at most 128 MiB of HBM per device.

```python
import math
import jax
import jax.numpy as jnp
import numpy as np
from jax import lax

D = 2048
HEAD_WIDTH = 128
QUERY_HEADS = 32
KEY_VALUE_HEADS = 2
FFE = 768
EXPERTS = 16
TOPK = 8
TOK_DEV = 32
SEQUENCE_TOKENS = 1024
CAP = 18
N_CTX = 4
N_EXP = 8


def attention_draw(key):
    base_key = jax.random.fold_in(key, 7)
    query_key, keyvalue_random_key = jax.random.split(base_key, 2)
    query_sample = jax.random.truncated_normal(query_key, -6.0, 6.0, (SEQUENCE_TOKENS, QUERY_HEADS, HEAD_WIDTH), jnp.float32)
    keyvalue_sample = jax.random.truncated_normal(keyvalue_random_key, -6.0, 6.0, (SEQUENCE_TOKENS, KEY_VALUE_HEADS, 2, HEAD_WIDTH), jnp.float32)
    return (query_sample.reshape(SEQUENCE_TOKENS, QUERY_HEADS * HEAD_WIDTH), keyvalue_sample.reshape(SEQUENCE_TOKENS, KEY_VALUE_HEADS * 2 * HEAD_WIDTH))


def draw_queries(key, part):
    return attention_draw(key)[0].astype(jnp.bfloat16)


def draw_keyvals(key, part):
    return attention_draw(key)[1].astype(jnp.bfloat16)


def shard_levels(rng, extent, cuts, low, high):
    factor_of = 1.0
    for position, blocks in cuts:
        draws = jax.random.uniform(jax.random.fold_in(jax.random.fold_in(rng, 6), position), (blocks,), jnp.float32, low / len(cuts), high / len(cuts))
        factor_of = factor_of * jnp.repeat(jnp.exp(draws), extent[position] // blocks).reshape((-1,) + (1,) * (len(extent) - 1 - position))
    return factor_of


def assign_block(key, own, number, rows, amount, top, limit, slope):
    ranking = jax.random.permutation(key, amount)
    packed, common = load_shares(amount, rows * top, limit, slope, True), load_shares(amount, rows * top, limit, slope, False)
    places = jnp.arange(amount)

    def named(tallies, offset_by):
        used = int((tallies > 0).sum())
        fixed = max(1, used // 4)
        moved = fixed + (places - fixed + offset_by * (used - fixed)) % max(1, amount - fixed)
        return jnp.zeros((amount,), jnp.int32).at[ranking[jnp.where(places < fixed, places, moved)]].set(jnp.asarray(tallies, jnp.int32))

    tallies = jnp.where(number % 4 == 0, named(packed, number // 4), named(common, number - number // 4 - 1))
    mixed = jax.random.permutation(jax.random.fold_in(own, 3), amount)
    donor, receiver = mixed[0:amount // 2 * 2:2], mixed[1:amount // 2 * 2:2]
    slack = jnp.minimum(tallies[donor] - 1, limit - tallies[receiver]) // 2
    slack = jnp.where((donor == ranking[0]) | (receiver == ranking[0]) | (tallies[receiver] == 0), 0, jnp.maximum(slack, 0))
    moved = jax.random.randint(jax.random.fold_in(own, 4), (amount // 2,), 0, 1 << 20) % (slack + 1)
    tallies = tallies.at[donor].add(-moved).at[receiver].add(moved)
    labels = jnp.searchsorted(jnp.cumsum(tallies), jnp.arange(rows * top), side="right").astype(jnp.int32)
    listing = labels.reshape(top, rows).T
    listing = listing[jax.random.permutation(jax.random.fold_in(own, 1), rows)]
    offset_by = jax.random.randint(jax.random.fold_in(own, 2), (rows, 1), 0, top)
    return jnp.take_along_axis(listing, (jnp.arange(top)[None, :] + offset_by) % top, axis=1)


def load_shares(count, total, limit, lean, full):
    loads = [(1 << 20) // math.isqrt(standing ** lean) + 1 for standing in range(1, count + 1)]
    largest = limit if full else min(limit, max(-(-total // count), total * loads[0] // sum(loads)))
    least = 1 if total - largest >= count - 1 else 0
    holding, surplus = [largest] + [least] * (count - 1), total - largest - least * (count - 1)
    while surplus > 0:
        candidates = [i for i in range(1, count) if holding[i] < largest] or [i for i in range(1, count) if holding[i] < limit]
        pool, left = sum([loads[i] for i in candidates]), surplus
        for i in candidates:
            extra = min(limit - holding[i], max(1, left * loads[i] // pool), surplus)
            holding[i] = holding[i] + extra
            surplus = surplus - extra
    return np.array(holding)


def gaussian(own_key, dims, spread, limit, cuts=(), kind=jnp.bfloat16):
    values = jax.random.normal(own_key, dims, jnp.float32) * spread
    if len(cuts) > 0:
        values = shard_levels(own_key, dims, cuts, -0.22, 0.18) * values
    return jnp.clip(values, min=-limit, max=limit).astype(kind)


def setup_inputs(seed: int = 0) -> dict:
    streams_of = jax.random.split(jax.random.key(seed), 11)
    hidden_in = gaussian(streams_of[0], (SEQUENCE_TOKENS, D), 1.0, 6.0, ((0, 32),))
    queries = draw_queries(jax.random.fold_in(streams_of[10], 71), 0)
    keyvals = draw_keyvals(jax.random.fold_in(streams_of[10], 71), 0)
    out_weight = gaussian(streams_of[3], (QUERY_HEADS * HEAD_WIDTH, D), (QUERY_HEADS * HEAD_WIDTH) ** -0.5, 0.09375, ((0, 8),))
    norm_gain = jnp.clip(1.0 + 0.1 * jax.random.normal(streams_of[4], (D,), jnp.float32), 0.5, 1.5)
    router_weight = gaussian(streams_of[5], (D, EXPERTS), D ** -0.5, 0.125)
    expert_gate_up = gaussian(streams_of[6], (EXPERTS, D, 2 * FFE), D ** -0.5, 0.125, ((0, 8), (1, 4)))
    expert_down = gaussian(streams_of[7], (EXPERTS, FFE, D), FFE ** -0.5, 0.21875, ((0, 8), (1, 4)))
    route_ids_keys = jax.random.split(jax.random.fold_in(streams_of[8], 1), SEQUENCE_TOKENS // TOK_DEV)
    route_ids_turns = jax.random.permutation(jax.random.fold_in(streams_of[8], 3), SEQUENCE_TOKENS // TOK_DEV)
    route_ids = jax.vmap(lambda own, number: assign_block(jax.random.fold_in(streams_of[8], 2), own, number, TOK_DEV, EXPERTS, TOPK, CAP, 2))(route_ids_keys, route_ids_turns).reshape((SEQUENCE_TOKENS, TOPK))
    upstream = gaussian(streams_of[9], (SEQUENCE_TOKENS, D), 1.0, 6.0, ((0, 32),))
    return {"hidden_in": hidden_in, "queries": queries, "keyvals": keyvals, "out_weight": out_weight, "norm_gain": norm_gain, "router_weight": router_weight, "expert_gate_up": expert_gate_up, "expert_down": expert_down, "route_ids": route_ids, "upstream": upstream}


norm_eps = 1e-06

def rounded(value):
    return lax.optimization_barrier(value.astype(jnp.bfloat16))

def reference(hidden_in, queries, keyvals, out_weight, norm_gain, router_weight, expert_gate_up, expert_down, route_ids, upstream):
    score_scale = HEAD_WIDTH ** (-0.5)
    group_width = QUERY_HEADS // KEY_VALUE_HEADS
    positions = jnp.arange(SEQUENCE_TOKENS, dtype=jnp.int32)
    allowed = positions[None, :] <= positions[:, None]

    def head_scores(head_index):
        query_rows = lax.dynamic_slice_in_dim(queries, head_index * HEAD_WIDTH, HEAD_WIDTH, 1)
        base_column = head_index // group_width * (2 * HEAD_WIDTH)
        key_rows = lax.dynamic_slice_in_dim(keyvals, base_column, HEAD_WIDTH, 1)
        value_rows = lax.dynamic_slice_in_dim(keyvals, base_column + HEAD_WIDTH, HEAD_WIDTH, 1)
        scores = jnp.dot(query_rows, key_rows.T, preferred_element_type=jnp.float32) * score_scale
        return (key_rows, value_rows, jnp.where(allowed, scores, -jnp.inf))

    def forward_head(head_index):
        key_rows, value_rows, scores = head_scores(head_index)
        row_max = lax.optimization_barrier(jnp.max(scores, axis=1))
        weights = jnp.exp(scores - row_max[:, None])
        row_sum = lax.optimization_barrier(jnp.sum(weights, axis=1))
        mixed = jnp.dot(weights.astype(jnp.bfloat16), value_rows, preferred_element_type=jnp.float32)
        return (rounded(mixed / row_sum[:, None]), row_max + jnp.log(row_sum))
    head_list = jnp.arange(QUERY_HEADS, dtype=jnp.int32)
    head_outs, log_totals = lax.map(forward_head, head_list)
    attention = jnp.transpose(head_outs, (1, 0, 2)).reshape(SEQUENCE_TOKENS, QUERY_HEADS * HEAD_WIDTH)
    projected = jnp.dot(attention, out_weight, preferred_element_type=jnp.float32)
    residual = hidden_in.astype(jnp.float32) + projected
    inv_rms = lax.rsqrt(lax.optimization_barrier(jnp.mean(residual * residual, axis=1, keepdims=True)) + norm_eps)
    normed = rounded(residual * inv_rms * norm_gain)
    logits = jnp.dot(normed, router_weight, preferred_element_type=jnp.float32)
    chosen = jnp.take_along_axis(logits, route_ids, axis=1)
    route_probs = jax.nn.softmax(chosen, axis=1)
    block_count = SEQUENCE_TOKENS // TOK_DEV
    route_blocks = route_ids.reshape(block_count, TOK_DEV, TOPK)
    expert_hit = route_blocks[..., None] == jnp.arange(EXPERTS, dtype=jnp.int32)
    hit_any = jnp.any(expert_hit, axis=2).astype(jnp.int32)
    earlier = jnp.cumsum(hit_any, axis=1) - hit_any
    slot_index = lax.optimization_barrier(jnp.sum(jnp.where(expert_hit, earlier[:, :, None, :], 0), axis=3))
    block_ids = jnp.arange(block_count, dtype=jnp.int32)
    ctx_ids = block_ids // N_EXP
    sub_ids = block_ids % N_EXP
    row_index = ((ctx_ids[:, None, None] * EXPERTS + route_blocks) * N_EXP + sub_ids[:, None, None]) * CAP + slot_index
    row_index = row_index.reshape(SEQUENCE_TOKENS * TOPK).astype(jnp.int32)
    row_total = N_CTX * EXPERTS * N_EXP * CAP
    spread_rows = jnp.repeat(normed, TOPK, axis=0)
    expert_inputs = jnp.zeros((row_total, D), jnp.bfloat16).at[row_index].set(spread_rows)
    expert_inputs = expert_inputs.reshape(N_CTX, EXPERTS, N_EXP * CAP, D)
    gate_up_full = expert_gate_up.astype(jnp.float32)
    down_full = expert_down.astype(jnp.float32)

    def expert_forward(inputs_here):
        gate_up = jnp.einsum('erd,edf->erf', inputs_here.astype(jnp.float32), gate_up_full)
        gate_part = gate_up[..., :FFE]
        up_part = gate_up[..., FFE:]
        activation = rounded(jax.nn.silu(gate_part) * up_part)
        expert_out = rounded(jnp.einsum('erf,efd->erd', activation.astype(jnp.float32), down_full))
        return (expert_out, gate_up, activation)
    expert_outs, gate_ups, activations = lax.map(expert_forward, expert_inputs)
    returned = expert_outs.reshape(row_total, D)[row_index].reshape(SEQUENCE_TOKENS, TOPK, D).astype(jnp.float32)
    mixture = jnp.einsum('tk,tkd->td', route_probs, returned)
    layer_out = (residual + mixture).astype(jnp.bfloat16)
    out_grad = upstream.astype(jnp.float32)
    row_grads = rounded(route_probs[:, :, None] * out_grad[:, None, :])
    prob_grads = lax.optimization_barrier(jnp.sum(returned * out_grad[:, None, :], axis=2))
    grad_inputs = jnp.zeros((row_total, D), jnp.bfloat16).at[row_index].set(row_grads.reshape(SEQUENCE_TOKENS * TOPK, D))
    grad_inputs = grad_inputs.reshape(N_CTX, EXPERTS, N_EXP * CAP, D)

    def expert_backward(totals, pieces):
        gate_up_sum, down_sum = totals
        inputs_here, grads_here, gate_up, activation = pieces
        gate_part = gate_up[..., :FFE]
        up_part = gate_up[..., FFE:]
        act_grad = jnp.einsum('erd,efd->erf', grads_here.astype(jnp.float32), down_full)
        sigmoid_gate = jax.nn.sigmoid(gate_part)
        gate_grad = act_grad * up_part * sigmoid_gate * (1.0 + gate_part * (1.0 - sigmoid_gate))
        up_grad = act_grad * gate_part * sigmoid_gate
        pair_grad = rounded(jnp.concatenate([gate_grad, up_grad], axis=-1))
        down_part = rounded(jnp.einsum('erf,erd->efd', activation.astype(jnp.float32), grads_here.astype(jnp.float32)))
        gate_up_part = rounded(jnp.einsum('erd,erf->edf', inputs_here.astype(jnp.float32), pair_grad.astype(jnp.float32)))
        rows_back = rounded(jnp.einsum('erf,edf->erd', pair_grad.astype(jnp.float32), gate_up_full))
        return ((gate_up_sum + gate_up_part.astype(jnp.float32), down_sum + down_part.astype(jnp.float32)), rows_back)
    start_totals = (jnp.zeros((EXPERTS, D, 2 * FFE), jnp.float32), jnp.zeros((EXPERTS, FFE, D), jnp.float32))
    (gate_up_grad, down_grad), rows_back = lax.scan(expert_backward, start_totals, (expert_inputs, grad_inputs, gate_ups, activations))
    input_rows = rows_back.reshape(row_total, D)[row_index].reshape(SEQUENCE_TOKENS, TOPK, D)
    expert_part = lax.optimization_barrier(jnp.sum(input_rows.astype(jnp.float32), axis=1))
    chosen_grad = route_probs * (prob_grads - lax.optimization_barrier(jnp.sum(route_probs * prob_grads, axis=1, keepdims=True)))
    hit_float = (route_ids[:, :, None] == jnp.arange(EXPERTS, dtype=jnp.int32)).astype(jnp.float32)
    logit_grad = jnp.einsum('tk,tke->te', chosen_grad, hit_float)
    router_grad = jnp.dot(normed.astype(jnp.float32).T, logit_grad, precision=lax.Precision.HIGHEST)
    normed_grad = expert_part + jnp.dot(logit_grad, router_weight.astype(jnp.float32).T, precision=lax.Precision.HIGHEST)
    gain_grad = lax.optimization_barrier(jnp.sum(normed_grad * residual * inv_rms, axis=0))
    inner_mean = lax.optimization_barrier(jnp.mean(residual * norm_gain * normed_grad, axis=1, keepdims=True))
    input_grad = rounded(out_grad + norm_gain * inv_rms * normed_grad - residual * inv_rms ** 3 * inner_mean)
    out_weight_grad = jnp.dot(attention.T, input_grad, preferred_element_type=jnp.float32)
    attention_grad = rounded(jnp.dot(input_grad, out_weight.T, preferred_element_type=jnp.float32))

    def backward_head(pieces):
        head_index, log_total, head_out = pieces
        key_rows, value_rows, scores = head_scores(head_index)
        head_grad = lax.dynamic_slice_in_dim(attention_grad, head_index * HEAD_WIDTH, HEAD_WIDTH, 1)
        attn_probs = jnp.exp(scores - log_total[:, None])
        prob_part = jnp.dot(head_grad, value_rows.T, preferred_element_type=jnp.float32)
        delta_rows = lax.optimization_barrier(jnp.sum(head_grad.astype(jnp.float32) * head_out.astype(jnp.float32), axis=1))
        score_grad = rounded(attn_probs * (prob_part - delta_rows[:, None]))
        return (score_scale * jnp.dot(score_grad, key_rows, preferred_element_type=jnp.float32)).astype(jnp.bfloat16)
    query_parts = lax.map(backward_head, (head_list, log_totals, head_outs))
    query_grad = jnp.transpose(query_parts, (1, 0, 2)).reshape(SEQUENCE_TOKENS, QUERY_HEADS * HEAD_WIDTH)
    return (layer_out, input_grad, query_grad, out_weight_grad, gate_up_grad, down_grad, router_grad, gain_grad)
```

```python
import jax
import jax.numpy as jnp
from jax import lax
from jax.sharding import PartitionSpec as P

HEAD_WIDTH = 128
QUERY_HEADS = 32
KEY_VALUE_HEADS = 2
FFE = 768
EXPERTS = 16


norm_eps = 1e-06


def per_device(
    hidden_in,
    queries,
    keyvals,
    out_weight,
    norm_gain,
    router_weight,
    expert_gate_up,
    expert_down,
    route_ids,
    upstream,
):
    exp_count = lax.axis_size("exp")
    ctx_index = lax.axis_index("ctx")
    exp_index = lax.axis_index("exp")
    tok_ctx = queries.shape[0]
    tok_dev = hidden_in.shape[0]
    local_heads = queries.shape[1] // HEAD_WIDTH
    local_experts = EXPERTS // exp_count
    score_scale = HEAD_WIDTH ** (-0.5)

    keyvalue_head = exp_index * local_heads // (QUERY_HEADS // KEY_VALUE_HEADS)
    own_block = lax.dynamic_slice_in_dim(keyvals, keyvalue_head * 2 * HEAD_WIDTH, 2 * HEAD_WIDTH, 1)
    all_kv = lax.all_gather(own_block, "ctx", axis=0, tiled=True)
    ids_block = lax.all_gather(route_ids, "exp", axis=0, tiled=True)
    upstream_block = lax.all_gather(upstream, "exp", axis=0, tiled=True)
    gate_up_full = lax.all_gather(expert_gate_up, "ctx", axis=1, tiled=True)
    down_full = lax.all_gather(expert_down, "ctx", axis=1, tiled=True)
    upstream_all = lax.all_gather(upstream_block, "ctx", axis=0, tiled=True)

    keys, values = all_kv[:, :HEAD_WIDTH], all_kv[:, HEAD_WIDTH:]
    query_pos = ctx_index * tok_ctx + jnp.arange(tok_ctx, dtype=jnp.int32)
    key_pos = jnp.arange(keys.shape[0], dtype=jnp.int32)
    allowed = key_pos[None, :] <= query_pos[:, None]

    def columns(array, head):
        return array[:, head * HEAD_WIDTH : (head + 1) * HEAD_WIDTH]

    def dot_t(a, b):
        return lax.dot_general(a, b, (((1,), (1,)), ((), ())), preferred_element_type=jnp.float32)

    def head_scores(head):
        return jnp.where(allowed, dot_t(columns(queries, head), keys) * score_scale, -jnp.inf)

    attention_heads, log_totals = [], []
    for head in range(local_heads):
        scores = head_scores(head)
        row_max = jnp.max(scores, axis=1, keepdims=True)
        weights = jnp.exp(scores - row_max)
        row_sum = jnp.sum(weights, axis=1, keepdims=True)
        mixed = jnp.dot(weights.astype(jnp.bfloat16), values, preferred_element_type=jnp.float32)
        attention_heads.append((mixed / row_sum).astype(jnp.bfloat16))
        log_totals.append(row_max + jnp.log(row_sum))
    attention_flat = jnp.concatenate(attention_heads, axis=1)
    attention_all = lax.all_gather(attention_flat, "ctx", axis=0, tiled=True)

    projected = lax.psum_scatter(
        jnp.dot(attention_flat, out_weight, preferred_element_type=jnp.float32).astype(jnp.bfloat16),
        "exp",
        scatter_dimension=0,
        tiled=True,
    ).astype(jnp.float32)
    residual = hidden_in.astype(jnp.float32) + projected
    inv_rms = lax.rsqrt(jnp.mean(residual * residual, axis=1, keepdims=True) + norm_eps)
    normed = (residual * inv_rms * norm_gain).astype(jnp.bfloat16)

    normed_block = lax.all_gather(normed, "exp", axis=0, tiled=True)
    normed_cols = lax.all_to_all(normed_block, "ctx", split_axis=1, concat_axis=0, tiled=True)
    logits = jnp.dot(normed_block, router_weight, preferred_element_type=jnp.float32)
    expert_ids = jnp.arange(EXPERTS, dtype=jnp.int32)
    hit_block = jnp.any(ids_block[:, :, None] == expert_ids, axis=1)
    masked = jnp.where(hit_block, logits, -jnp.inf)
    shifted = jnp.exp(masked - jnp.max(masked, axis=1, keepdims=True))
    probs_block = shifted / jnp.sum(shifted, axis=1, keepdims=True)
    probs_here = lax.dynamic_slice_in_dim(probs_block, exp_index * local_experts, local_experts, 1)
    probs_cols = probs_here.T[:, :, None]
    out_grad_block = upstream_block.astype(jnp.float32)
    row_grads = (probs_cols * out_grad_block[None]).astype(jnp.bfloat16)

    gate_up = jnp.einsum("td,edf->etf", normed_block, gate_up_full, preferred_element_type=jnp.float32)
    gate_part = gate_up[:, :, :FFE]
    up_part = gate_up[:, :, FFE:]
    sigmoid_gate = jax.nn.sigmoid(gate_part)
    activation = (gate_part * sigmoid_gate * up_part).astype(jnp.bfloat16)
    scaled_act = (probs_cols * activation.astype(jnp.float32)).astype(jnp.bfloat16)
    act_grad = jnp.einsum("etd,efd->etf", row_grads, down_full, preferred_element_type=jnp.float32)
    gate_grad = act_grad * up_part * sigmoid_gate * (1.0 + gate_part * (1.0 - sigmoid_gate))
    up_grad = act_grad * gate_part * sigmoid_gate
    pair_grad = jnp.concatenate([gate_grad, up_grad], axis=2).astype(jnp.bfloat16)
    pair_grad_all = lax.all_gather(pair_grad, "ctx", axis=1, tiled=True)
    rows_back = jnp.einsum("etf,edf->td", pair_grad, gate_up_full, preferred_element_type=jnp.float32)
    expert_part = lax.psum_scatter(
        rows_back.astype(jnp.bfloat16), "exp", scatter_dimension=0, tiled=True
    ).astype(jnp.float32)

    expert_out = jnp.einsum(
        "etf,efd->etd", activation, down_full, preferred_element_type=jnp.float32
    ).astype(jnp.bfloat16).astype(jnp.float32)
    prob_grads_here = jnp.sum(expert_out * out_grad_block[None], axis=2)
    prob_grads = lax.all_to_all(
        prob_grads_here, "exp", split_axis=1, concat_axis=0, tiled=True
    ).T
    mixture = lax.psum_scatter(
        jnp.sum(probs_cols * expert_out, axis=0).astype(jnp.bfloat16),
        "exp",
        scatter_dimension=0,
        tiled=True,
    ).astype(jnp.float32)
    layer_out = (residual + mixture).astype(jnp.bfloat16)

    act_rows = lax.all_to_all(
        jnp.swapaxes(scaled_act, 1, 2), "ctx", split_axis=1, concat_axis=2, tiled=True
    )
    down_grad = jnp.einsum("eft,td->efd", act_rows, upstream_all, preferred_element_type=jnp.float32)
    gate_up_grad = jnp.einsum(
        "td,etf->edf", normed_cols, pair_grad_all, preferred_element_type=jnp.float32
    )

    out_grad = upstream.astype(jnp.float32)
    probs = lax.dynamic_slice_in_dim(probs_block, exp_index * tok_dev, tok_dev, 0)
    logit_grad = probs * (prob_grads - jnp.sum(probs * prob_grads, axis=1, keepdims=True))
    router_term = jnp.einsum(
        "te,td->ed", logit_grad, normed.astype(jnp.float32), precision=lax.Precision.HIGHEST
    )
    normed_grad = expert_part + jnp.einsum(
        "te,de->td", logit_grad, router_weight.astype(jnp.float32), precision=lax.Precision.HIGHEST
    )
    gain_term = jnp.sum(normed_grad * residual * inv_rms, axis=0, keepdims=True)
    summed = lax.psum(jnp.concatenate([router_term, gain_term], axis=0), ("ctx", "exp"))
    router_grad, gain_grad = summed[:EXPERTS].T, summed[EXPERTS]
    inner_mean = jnp.mean(residual * norm_gain * normed_grad, axis=1, keepdims=True)
    input_grad = (
        out_grad + norm_gain * inv_rms * normed_grad - residual * inv_rms**3 * inner_mean
    ).astype(jnp.bfloat16)

    arriving = lax.all_gather(input_grad, "exp", axis=0, tiled=True)
    arriving_cols = lax.all_to_all(arriving, "ctx", split_axis=1, concat_axis=0, tiled=True)
    out_weight_grad = jnp.einsum(
        "tc,td->cd", attention_all, arriving_cols, preferred_element_type=jnp.float32
    )
    attention_grad = dot_t(arriving, out_weight).astype(jnp.bfloat16)

    query_grads = []
    for head in range(local_heads):
        grad_head = columns(attention_grad, head)
        delta = jnp.sum(
            grad_head.astype(jnp.float32) * attention_heads[head].astype(jnp.float32),
            axis=1,
            keepdims=True,
        )
        attn_probs = jnp.exp(head_scores(head) - log_totals[head])
        score_grad = (attn_probs * (dot_t(grad_head, values) - delta)).astype(jnp.bfloat16)
        query_acc = jnp.dot(score_grad, keys, preferred_element_type=jnp.float32)
        query_grads.append((score_scale * query_acc).astype(jnp.bfloat16))
    query_grad = jnp.concatenate(query_grads, axis=1)
    return (
        layer_out,
        input_grad,
        query_grad,
        out_weight_grad,
        gate_up_grad,
        down_grad,
        router_grad,
        gain_grad,
    )


def solution(mesh):
    return jax.shard_map(
        per_device,
        mesh=mesh,
        in_specs=(
            P(("ctx", "exp"), None),
            P("ctx", "exp"),
            P("ctx", None),
            P("exp", None),
            P(),
            P(),
            P("exp", "ctx", None),
            P("exp", "ctx", None),
            P(("ctx", "exp"), None),
            P(("ctx", "exp"), None),
        ),
        out_specs=(
            P(("ctx", "exp"), None),
            P(("ctx", "exp"), None),
            P("ctx", "exp"),
            P("exp", "ctx"),
            P("exp", "ctx", None),
            P("exp", "ctx", None),
            P(),
            P(),
        ),
        check_vma=False,
    )
```

```python
import jax
import jax.numpy as jnp
from jax import lax
from jax.sharding import PartitionSpec as P

D = 2048
HEAD_WIDTH = 128
QUERY_HEADS = 32
KEY_VALUE_HEADS = 2
FFE = 768
EXPERTS = 16
CAP = 18


norm_eps = 1e-06


def per_device(
    hidden_in,
    queries,
    keyvals,
    out_weight,
    norm_gain,
    router_weight,
    expert_gate_up,
    expert_down,
    route_ids,
    upstream,
):
    ctx_count = lax.axis_size("ctx")
    ctx_index = lax.axis_index("ctx")
    expert_number = lax.axis_index("exp")
    tok_ctx = queries.shape[0]
    local_heads = queries.shape[1] // HEAD_WIDTH
    score_scale = HEAD_WIDTH ** (-0.5)
    keyvalue_head = expert_number * local_heads // (QUERY_HEADS // KEY_VALUE_HEADS)
    own_block = lax.dynamic_slice_in_dim(keyvals, keyvalue_head * 2 * HEAD_WIDTH, 2 * HEAD_WIDTH, 1)
    all_kv = lax.all_gather(own_block, "ctx", axis=0, tiled=True)
    keys, values = all_kv[:, :HEAD_WIDTH], all_kv[:, HEAD_WIDTH:]
    query_pos = ctx_index * tok_ctx + jnp.arange(tok_ctx, dtype=jnp.int32)
    key_pos = jnp.arange(keys.shape[0], dtype=jnp.int32)
    allowed = key_pos[None, :] <= query_pos[:, None]

    def columns(array, head):
        return array[:, head * HEAD_WIDTH : (head + 1) * HEAD_WIDTH]

    def dot_t(a, b):
        return lax.dot_general(a, b, (((1,), (1,)), ((), ())), preferred_element_type=jnp.float32)

    def head_scores(head):
        return jnp.where(allowed, dot_t(columns(queries, head), keys) * score_scale, -jnp.inf)

    attention_heads, log_totals = [], []
    for head in range(local_heads):
        scores = head_scores(head)
        row_max = jnp.max(scores, axis=1, keepdims=True)
        weights = jnp.exp(scores - row_max)
        row_sum = jnp.sum(weights, axis=1, keepdims=True)
        mixed = jnp.dot(weights.astype(jnp.bfloat16), values, preferred_element_type=jnp.float32)
        attention_heads.append((mixed / row_sum).astype(jnp.bfloat16))
        log_totals.append(row_max + jnp.log(row_sum))
    attention_flat = jnp.concatenate(attention_heads, axis=1)
    rows_here = attention_flat
    projected = lax.psum_scatter(
        jnp.dot(rows_here, out_weight, preferred_element_type=jnp.float32).astype(jnp.bfloat16),
        "exp",
        scatter_dimension=0,
        tiled=True,
    ).astype(jnp.float32)
    residual = hidden_in.astype(jnp.float32) + projected
    inv_rms = lax.rsqrt(jnp.mean(residual * residual, axis=1, keepdims=True) + norm_eps)
    normed = (residual * inv_rms * norm_gain).astype(jnp.bfloat16)
    expert_hit = route_ids[:, :, None] == jnp.arange(EXPERTS, dtype=jnp.int32)
    hit_any = jnp.any(expert_hit, axis=1).astype(jnp.int32)
    earlier = jnp.cumsum(hit_any, axis=0) - hit_any
    slot_index = jnp.sum(jnp.where(expert_hit, earlier[:, None, :], 0), axis=2)
    flat_slot = route_ids * CAP + slot_index
    dispatch = (flat_slot[:, :, None] == jnp.arange(EXPERTS * CAP, dtype=jnp.int32)).astype(
        jnp.bfloat16
    )
    logits = jnp.dot(normed, router_weight, preferred_element_type=jnp.float32)
    chosen = jnp.sum(jnp.where(expert_hit, logits[:, None, :], 0.0), axis=2)
    route_probs = jax.nn.softmax(chosen, axis=1)
    outgoing = (
        jnp.einsum("tks,td->sd", dispatch, normed, preferred_element_type=jnp.float32)
        .astype(jnp.bfloat16)
        .reshape(EXPERTS, CAP, D)
    )
    arrived = lax.all_to_all(outgoing, "exp", split_axis=0, concat_axis=1, tiled=True)
    gate_up_full, down_full = (
        lax.all_gather(expert_gate_up, "ctx", axis=1, tiled=True),
        lax.all_gather(expert_down, "ctx", axis=1, tiled=True),
    )
    gate_up = jnp.einsum("erd,edf->erf", arrived, gate_up_full, preferred_element_type=jnp.float32)
    gate_part = gate_up[:, :, :FFE]
    up_part = gate_up[:, :, FFE:]
    activation = (jax.nn.silu(gate_part) * up_part).astype(jnp.bfloat16)
    expert_out = jnp.einsum(
        "erf,efd->erd", activation, down_full, preferred_element_type=jnp.float32
    ).astype(jnp.bfloat16)
    coming_back = lax.all_to_all(expert_out, "exp", split_axis=1, concat_axis=0, tiled=True)
    returned = jnp.einsum(
        "tks,sd->tkd",
        dispatch,
        coming_back.reshape(EXPERTS * CAP, D),
        preferred_element_type=jnp.float32,
    )
    mixture = jnp.sum(route_probs[:, :, None] * returned, axis=1)
    layer_out = (residual + mixture).astype(jnp.bfloat16)
    out_grad = upstream.astype(jnp.float32)
    row_grads = (route_probs[:, :, None] * out_grad[:, None, :]).astype(jnp.bfloat16)
    prob_grads = jnp.sum(returned * out_grad[:, None, :], axis=2)
    grad_outgoing = (
        jnp.einsum("tks,tkd->sd", dispatch, row_grads, preferred_element_type=jnp.float32)
        .astype(jnp.bfloat16)
        .reshape(EXPERTS, CAP, D)
    )
    grad_arrived = lax.all_to_all(grad_outgoing, "exp", split_axis=0, concat_axis=1, tiled=True)
    gate_up_back, down_back = (gate_up_full, down_full)
    act_grad = jnp.einsum(
        "erd,efd->erf", grad_arrived, down_back, preferred_element_type=jnp.float32
    )
    sigmoid_gate = jax.nn.sigmoid(gate_part)
    gate_grad = act_grad * up_part * sigmoid_gate * (1.0 + gate_part * (1.0 - sigmoid_gate))
    up_grad = act_grad * gate_part * sigmoid_gate
    pair_grad = jnp.concatenate([gate_grad, up_grad], axis=2).astype(jnp.bfloat16)
    down_term = jnp.einsum(
        "erf,erd->efd", activation, grad_arrived, preferred_element_type=jnp.float32
    )
    gate_up_term = jnp.einsum(
        "erd,erf->edf", arrived, pair_grad, preferred_element_type=jnp.float32
    )
    rows_back = jnp.einsum(
        "erf,edf->erd", pair_grad, gate_up_back, preferred_element_type=jnp.float32
    ).astype(jnp.bfloat16)
    grad_returned = lax.all_to_all(rows_back, "exp", split_axis=1, concat_axis=0, tiled=True)
    gate_up_grad, down_grad = (
        lax.psum_scatter(
            gate_up_term.astype(jnp.bfloat16), "ctx", scatter_dimension=1, tiled=True
        ).astype(jnp.float32),
        lax.psum_scatter(
            down_term.astype(jnp.bfloat16), "ctx", scatter_dimension=1, tiled=True
        ).astype(jnp.float32),
    )
    expert_part = jnp.einsum(
        "tks,sd->td",
        dispatch,
        grad_returned.reshape(EXPERTS * CAP, D),
        preferred_element_type=jnp.float32,
    )
    chosen_grad = route_probs * (
        prob_grads - jnp.sum(route_probs * prob_grads, axis=1, keepdims=True)
    )
    logit_grad = jnp.sum(jnp.where(expert_hit, chosen_grad[:, :, None], 0.0), axis=1)
    normed_float = normed.astype(jnp.float32)
    router_term = jnp.einsum("te,td->ed", logit_grad, normed_float, precision=lax.Precision.HIGHEST)
    normed_grad = expert_part + jnp.einsum(
        "te,de->td", logit_grad, router_weight.astype(jnp.float32), precision=lax.Precision.HIGHEST
    )
    gain_term = jnp.sum(normed_grad * residual * inv_rms, axis=0, keepdims=True)
    summed = lax.psum(jnp.concatenate([router_term, gain_term], axis=0), ("ctx", "exp"))
    router_grad, gain_grad = summed[:EXPERTS].T, summed[EXPERTS]
    inner_mean = jnp.mean(residual * norm_gain * normed_grad, axis=1, keepdims=True)
    input_grad = (
        out_grad + norm_gain * inv_rms * normed_grad - residual * inv_rms**3 * inner_mean
    ).astype(jnp.bfloat16)
    arriving = lax.all_gather(input_grad, "exp", axis=0, tiled=True)
    rows_here = attention_flat
    weight_part = jnp.einsum("tc,td->cd", rows_here, arriving, preferred_element_type=jnp.float32)
    new_rows = jnp.einsum("td,cd->tc", arriving, out_weight, preferred_element_type=jnp.float32)
    attn_part = new_rows
    weight_part, attn_part = (weight_part, attn_part)
    out_weight_grad = lax.psum_scatter(
        weight_part.astype(jnp.bfloat16), "ctx", scatter_dimension=1, tiled=True
    ).astype(jnp.float32)
    attention_grad = attn_part.astype(jnp.bfloat16)
    query_grads = []
    for head in range(local_heads):
        grad_head = columns(attention_grad, head)
        delta = jnp.sum(
            grad_head.astype(jnp.float32) * attention_heads[head].astype(jnp.float32),
            axis=1,
            keepdims=True,
        )
        attn_probs = jnp.exp(head_scores(head) - log_totals[head])
        score_grad = (attn_probs * (dot_t(grad_head, values) - delta)).astype(jnp.bfloat16)
        query_acc = jnp.dot(score_grad, keys, preferred_element_type=jnp.float32)
        query_grads.append((score_scale * query_acc).astype(jnp.bfloat16))
    query_grad = jnp.concatenate(query_grads, axis=1)
    return (
        layer_out,
        input_grad,
        query_grad,
        out_weight_grad,
        gate_up_grad,
        down_grad,
        router_grad,
        gain_grad,
    )


def solution(mesh):
    return jax.shard_map(
        per_device,
        mesh=mesh,
        in_specs=(
            P(("ctx", "exp"), None),
            P("ctx", "exp"),
            P("ctx", None),
            P("exp", None),
            P(),
            P(),
            P("exp", "ctx", None),
            P("exp", "ctx", None),
            P(("ctx", "exp"), None),
            P(("ctx", "exp"), None),
        ),
        out_specs=(
            P(("ctx", "exp"), None),
            P(("ctx", "exp"), None),
            P("ctx", "exp"),
            P("exp", "ctx"),
            P("exp", "ctx", None),
            P("exp", "ctx", None),
            P(),
            P(),
        ),
        check_vma=False,
    )
```
